32 devices in a mesh: dp: 2 (over y), row: 4 (over x, core), col: 4 (over z).
Axes of the slice: x: 2, y: 2, z: 4, core: 2. Of those that a mesh axis runs over, the one named last changes fastest.
Arguments:
- tokens: bfloat16 [2048, 4096], P(('col', 'row'), 'dp'), may hold values from -6 to 6
- segments: int32 [4096], P('dp'), may hold values from 0 to 12, never falling along the last dimension, each value on 1 to 800 neighbouring positions
- channel_table: bfloat16 [14, 2048], P(None, ('col', 'row')), may hold values from -7.6 to 2
- w_recept: bfloat16 [4, 512, 2048], P(None, 'row', 'col'), may hold values from -0.125 to 0.125
- w_key: bfloat16 [4, 512, 2048], P(None, 'row', 'col'), may hold values from -0.125 to 0.125
- w_value: bfloat16 [4, 512, 2048], P(None, 'row', 'col'), may hold values from -0.125 to 0.125
- w_gate: bfloat16 [4, 512, 2048], P(None, 'row', 'col'), may hold values from -0.125 to 0.125
- w_output: bfloat16 [4, 512, 2048], P(None, 'row', 'col'), may hold values from -0.125 to 0.125
- ffn_key: bfloat16 [4, 1792, 2048], P(None, 'row', 'col'), may hold values from -0.125 to 0.125
- ffn_value: bfloat16 [4, 512, 7168], P(None, 'row', 'col'), may hold values from -0.0625 to 0.0625
- ffn_recept: bfloat16 [4, 512, 2048], P(None, 'row', 'col'), may hold values from -0.125 to 0.125
- cotangent: bfloat16 [2048, 4096], P(('col', 'row'), 'dp'), may hold values from -6 to 6
Outputs:
- mixed: bfloat16 [2048, 4096], P(('col', 'row'), 'dp')
- grad_tokens: float32 [2048, 4096], P(('col', 'row'), 'dp')
- grad_table: float32 [14, 2048], P(None, ('col', 'row'))
- grad_recept: float32 [4, 512, 2048], P(None, 'row', 'col')
- grad_key: float32 [4, 512, 2048], P(None, 'row', 'col')
- grad_value: float32 [4, 512, 2048], P(None, 'row', 'col')
- grad_gate: float32 [4, 512, 2048], P(None, 'row', 'col')
- grad_output: float32 [4, 512, 2048], P(None, 'row', 'col')
- grad_ffn_key: float32 [4, 1792, 2048], P(None, 'row', 'col')
- grad_ffn_value: float32 [4, 512, 7168], P(None, 'row', 'col')
- grad_ffn_recept: float32 [4, 512, 2048], P(None, 'row', 'col')
The draws below stay inside these ranges and needn't reach their ends.
Inputs may be any that keep to these rules, and one draw needn't show every extreme that they name: `segments`: numbers never fall along the tokens; each document holds 1 to 800 tokens and one holds exactly 800; a document may run past a sequence's end.
All inputs are finite; a program needn't handle non-finite values.
Results may differ from the reference program's by a relative error of at most 0.019.
Values may be sent and summed in bfloat16 or wider, within the bound.
No kernel may reach another device: no remote copies, remote signals or barrier semaphores. Data moves between devices by JAX's collectives and lax.ppermute only.
A program may use at most 192 MiB of HBM per device.

```python
import math
import jax
import jax.numpy as jnp
import numpy as np
from jax import lax

D = 2048
FF = 7168
CHANNELS_PER_ATTN = 64
NPAR = 14
SEQ = 1024
DOC = 800
TOK_DP = 2048
TOKENS = 4096
NDOCS = 13
N_COL = 4


def draw_channel_table(key, part):
    lower_ends = jnp.array([0.5, -0.3, 0.05, 0.05, 0.05, 0.05, -7.6, -2.0, 0.5, -0.3, 0.5, -0.3, 0.05, 0.05], jnp.float32)
    upper_ends = jnp.array([1.5, 0.3, 0.95, 0.95, 0.95, 0.95, -3.4, 2.0, 1.5, 0.3, 1.5, 0.3, 0.95, 0.95], jnp.float32)
    uniform_draw = jax.random.uniform(key, (NPAR, D), jnp.float32)
    return (lower_ends[:, None] + (upper_ends - lower_ends)[:, None] * uniform_draw).astype(jnp.bfloat16)


def level_of(key, shape, cuts, least, high):
    level, own = 1.0, jax.random.fold_in(key, 6)
    for axis_at, shards_of in cuts:
        heights = jnp.exp(jax.random.uniform(jax.random.fold_in(own, axis_at), (shards_of,), jnp.float32, least / len(cuts), high / len(cuts)))
        level = level * jnp.repeat(heights, shape[axis_at] // shards_of).reshape([-1 if axis == axis_at else 1 for axis in range(len(shape))])
    return level


def profile(amount, total, reach, lean):
    portions = [(1 << 20) // math.isqrt(grade ** lean) + 1 for grade in range(2, amount + 1)]
    rest, given = total - reach - (amount - 1), [1] * (amount - 1)
    while rest > 0:
        movable = [i for i in range(amount - 1) if given[i] < reach]
        pool, left = sum([portions[i] for i in movable]), rest
        for i in movable:
            addition = min(reach - given[i], max(1, left * portions[i] // pool), rest)
            given[i] = given[i] + addition
            rest = rest - addition
    return np.array([reach] + given)


def uneven_parts(key, number_of, total, limit, skew):
    if number_of == 2:
        one = jax.random.randint(key, (), max(1, total - limit), min(limit, total - 1) + 1)
        return jnp.stack([one, total - one])
    lengths = jnp.asarray(profile(number_of, total, limit, skew), jnp.int32)
    couples = (number_of - 1) // 2
    giver, taker = lengths[1:1 + 2 * couples:2], lengths[2:2 + 2 * couples:2]
    margin = jnp.minimum(giver - 1, limit - taker)
    passed = jax.random.randint(jax.random.fold_in(key, 1), (couples,), 0, 1 << 20) % (margin + 1)
    lengths = lengths.at[1:1 + 2 * couples:2].set(giver - passed).at[2:2 + 2 * couples:2].set(taker + passed)
    return lengths[jax.random.permutation(jax.random.fold_in(key, 2), number_of)]


def normal_values(key, extent, deviation, limit, shards=(), held_as=jnp.bfloat16):
    drawn = deviation * jax.random.normal(key, extent, jnp.float32)
    if shards:
        drawn = drawn * level_of(key, extent, shards, -0.22, 0.18)
    return jnp.clip(drawn, -limit, limit).astype(held_as)


def setup_inputs(seed: int = 0) -> dict:
    splits = jax.random.split(jax.random.key(seed), 13)
    tokens = normal_values(splits[0], (D, TOKENS), 1.0, 6.0, ((0, 16), (1, 2)))
    segments = jnp.searchsorted(jnp.cumsum(uneven_parts(splits[1], NDOCS, TOKENS, DOC, 1)), jnp.arange(TOKENS), side="right").astype(jnp.int32)
    channel_table = draw_channel_table(jax.random.fold_in(splits[12], 71), 0)
    w_recept = normal_values(splits[3], (N_COL, D // N_COL, D), D ** -0.5, 0.125, ((1, 4), (2, 4)))
    w_key = normal_values(splits[4], (N_COL, D // N_COL, D), D ** -0.5, 0.125, ((1, 4), (2, 4)))
    w_value = normal_values(splits[5], (N_COL, D // N_COL, D), D ** -0.5, 0.125, ((1, 4), (2, 4)))
    w_gate = normal_values(splits[6], (N_COL, D // N_COL, D), D ** -0.5, 0.125, ((1, 4), (2, 4)))
    w_output = normal_values(splits[7], (N_COL, D // N_COL, D), D ** -0.5, 0.125, ((1, 4), (2, 4)))
    ffn_key = normal_values(splits[8], (N_COL, FF // N_COL, D), D ** -0.5, 0.125, ((1, 4), (2, 4)))
    ffn_value = normal_values(splits[9], (N_COL, D // N_COL, FF), FF ** -0.5, 0.0625, ((1, 4), (2, 4)))
    ffn_recept = normal_values(splits[10], (N_COL, D // N_COL, D), D ** -0.5, 0.125, ((1, 4), (2, 4)))
    cotangent = normal_values(splits[11], (D, TOKENS), 1.0, 6.0, ((0, 16), (1, 2)))
    return dict(tokens=tokens, segments=segments, channel_table=channel_table, w_recept=w_recept, w_key=w_key, w_value=w_value, w_gate=w_gate, w_output=w_output, ffn_key=ffn_key, ffn_value=ffn_value, ffn_recept=ffn_recept, cotangent=cotangent)


@jax.custom_vjp
def low(v):
    return lax.optimization_barrier(v.astype(jnp.bfloat16)).astype(jnp.float32)

@jax.custom_vjp
def low_back(v):
    return v

def low_keep(v):
    return (low(v), None)

def low_pass(kept, grad):
    return (grad,)

def back_keep(v):
    return (v, None)

def back_low(kept, grad):
    return (low(grad),)
low.defvjp(low_keep, low_pass)
low_back.defvjp(back_keep, back_low)
exact_mode = lax.Precision.HIGHEST
norm_eps = 1e-05
group_eps = 0.00064
head_divisor = 8.0
block_len = 64

def matmul_exact(left, right):
    return jnp.dot(left, right, precision=exact_mode, preferred_element_type=jnp.float32)

def layer_norm(payload_entries, gain, bias):
    center = lax.optimization_barrier(jnp.mean(payload_entries, axis=1, keepdims=True))
    spread = lax.optimization_barrier(jnp.mean(jnp.square(payload_entries - center), axis=1, keepdims=True))
    return (payload_entries - center) * lax.rsqrt(spread + norm_eps) * gain + bias

def shift_down(payload_entries, handed_onward):
    earlier = jnp.concatenate([jnp.zeros_like(payload_entries[:1]), payload_entries[:-1]], axis=0)
    return earlier * handed_onward[:, None]

def mixed_input(normed, shifted, coeff):
    return low(normed * coeff + shifted * (1.0 - coeff))

def attention_mixing_segmented(ongoing_memory_matrix, segment_portions, logarithmic_fading_speed, extra_current_coeffs):
    acceptance_entries, lookup_sources, payload_entries, beginning_markers = segment_portions
    positions = jnp.arange(block_len, dtype=jnp.int32)
    start_marks = jnp.where(beginning_markers > 0.5, positions, -1)
    last_start = lax.cummax(start_marks, axis=0)
    steps_in = positions.astype(jnp.float32)[:, None, None]
    scaled_r = acceptance_entries * jnp.exp(logarithmic_fading_speed[None] * steps_in)
    scaled_k = lookup_sources * jnp.exp(-logarithmic_fading_speed[None] * (steps_in + 1.0))
    end_k = lookup_sources * jnp.exp(logarithmic_fading_speed[None] * (block_len - 1.0 - steps_in))
    allowed = (positions[:, None] > positions[None, :]) & (last_start[:, None] <= positions[None, :])
    scores = jnp.einsum('thi,shi->hts', scaled_r, scaled_k, precision=exact_mode)
    scores = jnp.where(allowed[None], scores, 0.0)
    intra_term = jnp.einsum('hts,shj->thj', scores, payload_entries, precision=exact_mode)
    diagonal_contribution = lax.optimization_barrier(jnp.sum(acceptance_entries * extra_current_coeffs[None] * lookup_sources, axis=2, keepdims=True)) * payload_entries
    open_start = (last_start < 0).astype(jnp.float32)
    inter_term = jnp.einsum('thi,hij->thj', scaled_r, ongoing_memory_matrix, precision=exact_mode) * open_start[:, None, None]
    tail_mask = (positions >= last_start[block_len - 1]).astype(jnp.float32)
    fresh_sum = jnp.einsum('shi,shj->hij', end_k * tail_mask[:, None, None], payload_entries, precision=exact_mode)
    carried = ongoing_memory_matrix * jnp.exp(logarithmic_fading_speed * block_len)[:, :, None] * open_start[block_len - 1] + fresh_sum
    return (carried, intra_term + diagonal_contribution + inter_term)

def attention_mixing_complete(acceptance_entries, lookup_sources, payload_entries, beginning_markers, logarithmic_fading_speed, extra_current_coeffs):
    block_count = acceptance_entries.shape[0] // block_len

    def reshaped(array_in):
        return array_in.reshape((block_count, block_len) + array_in.shape[1:])
    checked_outcome = jax.checkpoint(attention_mixing_segmented)

    def step_fn(ongoing_memory_matrix, segment_portions):
        return checked_outcome(ongoing_memory_matrix, segment_portions, logarithmic_fading_speed, extra_current_coeffs)
    initial = jnp.zeros((logarithmic_fading_speed.shape[0], logarithmic_fading_speed.shape[1], logarithmic_fading_speed.shape[1]), jnp.float32)
    unused, outputs = lax.scan(step_fn, initial, (reshaped(acceptance_entries), reshaped(lookup_sources), reshaped(payload_entries), reshaped(beginning_markers)))
    return outputs.reshape(acceptance_entries.shape)

def layer_forward(tokens_in, parameter_catalog, weights, handed_onward):
    w_recept, w_key, w_value, w_gate, w_output, ffn_key, ffn_value, ffn_recept = weights
    token_count = tokens_in.shape[0]
    attention_group_total = D // CHANNELS_PER_ATTN
    normed = layer_norm(tokens_in, parameter_catalog[0], parameter_catalog[1])
    shifted = shift_down(normed, handed_onward)
    acceptance_entries = low_back(matmul_exact(mixed_input(normed, shifted, parameter_catalog[2]), w_recept))
    lookup_mapped = low_back(matmul_exact(mixed_input(normed, shifted, parameter_catalog[3]), w_key))
    payload_mapped = low_back(matmul_exact(mixed_input(normed, shifted, parameter_catalog[4]), w_value))
    gate_pre = low_back(matmul_exact(mixed_input(normed, shifted, parameter_catalog[5]), w_gate))

    def divide_attention_groups(array_in):
        return array_in.reshape(token_count, attention_group_total, CHANNELS_PER_ATTN)
    logarithmic_fading_speed = (-jnp.exp(parameter_catalog[6])).reshape(attention_group_total, CHANNELS_PER_ATTN)
    extra_current_coeffs = parameter_catalog[7].reshape(attention_group_total, CHANNELS_PER_ATTN)
    combined_attention_groups = attention_mixing_complete(divide_attention_groups(acceptance_entries), divide_attention_groups(lookup_mapped), divide_attention_groups(payload_mapped), 1.0 - handed_onward, logarithmic_fading_speed, extra_current_coeffs) / head_divisor
    center = lax.optimization_barrier(jnp.mean(combined_attention_groups, axis=2, keepdims=True))
    spread = lax.optimization_barrier(jnp.mean(jnp.square(combined_attention_groups - center), axis=2, keepdims=True))
    grouped = ((combined_attention_groups - center) * lax.rsqrt(spread + group_eps)).reshape(token_count, D)
    gated_out = low((grouped * parameter_catalog[8] + parameter_catalog[9]) * jax.nn.silu(gate_pre))
    residual = tokens_in + low_back(matmul_exact(gated_out, w_output))
    normed_two = layer_norm(residual, parameter_catalog[10], parameter_catalog[11])
    shifted_two = shift_down(normed_two, handed_onward)
    hidden_pre = low_back(matmul_exact(mixed_input(normed_two, shifted_two, parameter_catalog[12]), ffn_key))
    recept_pre = low_back(matmul_exact(mixed_input(normed_two, shifted_two, parameter_catalog[13]), ffn_recept))
    activated = low(jnp.square(jax.nn.relu(hidden_pre)))
    valued_two = low_back(matmul_exact(activated, ffn_value))
    return residual + jax.nn.sigmoid(recept_pre) * valued_two

def reference(tokens, segments, channel_table, w_recept, w_key, w_value, w_gate, w_output, ffn_key, ffn_value, ffn_recept, cotangent):
    supplied = (w_recept, w_key, w_value, w_gate, w_output, ffn_key, ffn_value, ffn_recept)
    weights = tuple((weight.astype(jnp.float32).reshape(-1, weight.shape[2]).T for weight in supplied))
    parameter_catalog = channel_table.astype(jnp.float32)
    group_count = TOKENS // TOK_DP
    tokens_grouped = tokens.astype(jnp.float32).T.reshape(group_count, TOK_DP, D)
    segments_grouped = segments.reshape(group_count, TOK_DP)
    upstream_grouped = cotangent.astype(jnp.float32).T.reshape(group_count, TOK_DP, D)

    def one_group(totals, segment_portions):
        tokens_in, segment_ids, upstream = segment_portions
        positions = jnp.arange(TOK_DP, dtype=jnp.int32)
        earlier = jnp.concatenate([segment_ids[:1], segment_ids[:-1]])
        beginning_markers = (positions % SEQ == 0) | (segment_ids != earlier)
        handed_onward = 1.0 - beginning_markers.astype(jnp.float32)

        def closed(tokens_x, table_x, weights_x):
            return layer_forward(tokens_x, table_x, weights_x, handed_onward)
        result, pullback = jax.vjp(closed, tokens_in, parameter_catalog, weights)
        grad_in, grad_tab, grad_weights = pullback(upstream)
        totals = jax.tree.map(jnp.add, totals, (grad_tab, grad_weights))
        return (totals, (result.astype(jnp.bfloat16), grad_in))
    zeros_start = jax.tree.map(jnp.zeros_like, (parameter_catalog, weights))
    totals, stacked = lax.scan(one_group, zeros_start, (tokens_grouped, segments_grouped, upstream_grouped))
    grad_tab, grad_weights = totals
    results, grads_in = stacked
    shaped = [grad.T.reshape(weight.shape) for grad, weight in zip(grad_weights, supplied)]
    return (results.reshape(TOKENS, D).T, grads_in.reshape(TOKENS, D).T, grad_tab, shaped[0], shaped[1], shaped[2], shaped[3], shaped[4], shaped[5], shaped[6], shaped[7])
```

```python
import functools

import jax
import jax.numpy as jnp
from jax import lax
from jax.experimental import pallas as pl
from jax.experimental.pallas import tpu as pltpu
from jax.sharding import Mesh, PartitionSpec as P

HEAD = 64
SEQ = 1024
NPAR = 14
CHUNK = 128
LANES = 128
F32 = jnp.float32
BF16 = jnp.bfloat16
norm_eps = 1e-05
group_eps = 0.00064
head_divisor = 8.0


NN = (((1,), (0,)), ((), ()))
NT = (((1,), (1,)), ((), ()))
TN = (((0,), (0,)), ((), ()))


def split(a):
    hi = a.astype(BF16)
    return hi, (a - hi.astype(F32)).astype(BF16)


def mm3(a, b, dims):
    (ah, al), (bh, bl) = a, b
    one = functools.partial(lax.dot_general, dimension_numbers=dims, preferred_element_type=F32)
    return one(ah, bh) + (one(ah, bl) + one(al, bh))


def rows_of(pair, h):
    return tuple(part[h * HEAD : (h + 1) * HEAD] for part in pair)


def per_head(value, heads):
    return value.reshape(heads, HEAD, value.shape[-1])


def decay_tables(tab_ref):
    lw = tab_ref[:, 0:1]
    tau = lax.broadcasted_iota(jnp.int32, (1, CHUNK), 1).astype(F32)
    mid = CHUNK // 2
    er = jnp.exp(lw * (tau - mid))
    ek = jnp.exp(-lw * (tau + 1.0 - mid))
    eend = jnp.exp(lw * (CHUNK - 1.0 - tau))
    ein = jnp.exp(lw * tau)
    return er, ek, eend, ein


def chunk_masks(ls_ref, base):
    ls = ls_ref[...]
    s_at = lax.broadcasted_iota(jnp.int32, (CHUNK, CHUNK), 0) + base
    t_at = lax.broadcasted_iota(jnp.int32, (CHUNK, CHUNK), 1) + base
    allowed = (s_at < t_at) & (s_at >= ls)
    opened = (ls < base).astype(F32)
    last = jnp.max(ls, axis=1, keepdims=True)
    tail = ((lax.broadcasted_iota(jnp.int32, (1, CHUNK), 1) + base) >= last).astype(F32)
    open_end = (last < base).astype(F32)
    return allowed, opened, tail, open_end


def diagonal_blocks(width):
    a = lax.broadcasted_iota(jnp.int32, (width, width), 0) // HEAD
    b = lax.broadcasted_iota(jnp.int32, (width, width), 1) // HEAD
    return a == b


def mix_forward_kernel(heads, r_ref, k_ref, v_ref, g_ref, tab_ref, row_ref, ls_ref,
                       z_ref, o_ref, st_ref, state):
    width = heads * HEAD
    base = pl.program_id(0) * CHUNK

    @pl.when(pl.program_id(0) == 0)
    def _():
        state[...] = jnp.zeros_like(state)

    st = state[...]
    st_ref[0] = st
    er, ek, eend, ein = decay_tables(tab_ref)
    allowed, opened, tail, open_end = chunk_masks(ls_ref, base)
    r, k, v = r_ref[...], k_ref[...], v_ref[...]
    rt, kt, vp = split(r * er), split(k * ek), split(v)
    outs = []
    for h in range(heads):
        scores = mm3(rows_of(kt, h), rows_of(rt, h), TN)
        scores = split(jnp.where(allowed, scores, 0.0))
        outs.append(mm3(rows_of(vp, h), scores, NN))
    o = jnp.concatenate(outs, axis=0)
    o = o + mm3(split(st), split(r * (ein * opened)), NN)
    ruk = jnp.sum(per_head(r * tab_ref[:, 1:2] * k, heads), axis=1, keepdims=True)
    o = o + (per_head(v, heads) * ruk).reshape(width, CHUNK)
    fresh = mm3(vp, split(k * (eend * tail)), NT)
    state[...] = st * (jnp.exp(row_ref[0:1, :] * CHUNK) * open_end) + jnp.where(
        diagonal_blocks(width), fresh, 0.0
    )
    o_ref[...] = o
    x = per_head(o / head_divisor, heads)
    center = jnp.mean(x, axis=1, keepdims=True)
    spread = jnp.mean(jnp.square(x - center), axis=1, keepdims=True)
    y = ((x - center) * lax.rsqrt(spread + group_eps)).reshape(width, CHUNK)
    g = g_ref[...]
    z_ref[...] = ((y * tab_ref[:, 2:3] + tab_ref[:, 3:4]) * (g * jax.nn.sigmoid(g))).astype(BF16)


def mix_backward_kernel(heads, r_ref, k_ref, v_ref, g_ref, o_ref, dz_ref, st_ref, tab_ref, row_ref,
                        ls_ref, dr_ref, dk_ref, dv_ref, dg_ref, acc_ref, row_acc_ref, dstate):
    width = heads * HEAD
    base = (pl.num_programs(0) - 1 - pl.program_id(0)) * CHUNK

    @pl.when(pl.program_id(0) == 0)
    def _():
        dstate[...] = jnp.zeros_like(dstate)
        acc_ref[...] = jnp.zeros_like(acc_ref)
        row_acc_ref[...] = jnp.zeros_like(row_acc_ref)

    u, gain, bias = tab_ref[:, 1:2], tab_ref[:, 2:3], tab_ref[:, 3:4]
    x = per_head(o_ref[...] / head_divisor, heads)
    center = jnp.mean(x, axis=1, keepdims=True)
    spread = jnp.mean(jnp.square(x - center), axis=1, keepdims=True)
    inverse = lax.rsqrt(spread + group_eps)
    xh = (x - center) * inverse
    xh_flat = xh.reshape(width, CHUNK)
    g, dz = g_ref[...], dz_ref[...]
    sg = jax.nn.sigmoid(g)
    dy = dz * (g * sg)
    dg_ref[...] = (dz * (xh_flat * gain + bias) * (sg * (1.0 + g * (1.0 - sg)))).astype(BF16)
    acc_ref[2] += dy * xh_flat
    acc_ref[3] += dy
    dxh = per_head(dy * gain, heads)
    dx = inverse * (
        dxh
        - jnp.mean(dxh, axis=1, keepdims=True)
        - xh * jnp.mean(dxh * xh, axis=1, keepdims=True)
    )
    do = dx.reshape(width, CHUNK) / head_divisor
    er, ek, eend, ein = decay_tables(tab_ref)
    allowed, opened, tail, open_end = chunk_masks(ls_ref, base)
    r, k, v = r_ref[...], k_ref[...], v_ref[...]
    st, dst = st_ref[0], dstate[...]
    rt, kt, vp, dop = split(r * er), split(k * ek), split(v), split(do)
    dst_p = split(dst)
    dr_in, dk_in, dv_in = [], [], []
    for h in range(heads):
        rt_h, kt_h, v_h, do_h = rows_of(rt, h), rows_of(kt, h), rows_of(vp, h), rows_of(dop, h)
        a = split(jnp.where(allowed, mm3(v_h, do_h, TN), 0.0))
        q = split(jnp.where(allowed, mm3(kt_h, rt_h, TN), 0.0))
        dr_in.append(mm3(kt_h, a, NN))
        dk_in.append(mm3(rt_h, a, NT))
        dv_in.append(mm3(do_h, q, NT))
    ein_open = ein * opened
    end_tail = eend * tail
    dr = jnp.concatenate(dr_in, axis=0) * er + mm3(split(st), dop, TN) * ein_open
    dk = jnp.concatenate(dk_in, axis=0) * ek + mm3(dst_p, vp, TN) * end_tail
    dv = jnp.concatenate(dv_in, axis=0) + mm3(dst_p, split(k * end_tail), NN)
    fresh = mm3(dop, split(r * ein_open), NT)
    dst_new = dst * (jnp.exp(row_ref[0:1, :] * CHUNK) * open_end) + jnp.where(
        diagonal_blocks(width), fresh, 0.0
    )
    dstate[...] = dst_new
    tau = lax.broadcasted_iota(jnp.int32, (1, CHUNK), 1).astype(F32)
    acc_ref[0] += tau * (r * dr) - (tau + 1.0) * (k * dk)
    row_acc_ref[0:1, :] += CHUNK * jnp.sum(st * dst_new, axis=0, keepdims=True)
    vd = jnp.sum(per_head(v * do, heads), axis=1, keepdims=True)
    vd = jnp.broadcast_to(vd, (heads, HEAD, CHUNK)).reshape(width, CHUNK)
    acc_ref[1] += r * k * vd
    ruk = jnp.sum(per_head(r * u * k, heads), axis=1, keepdims=True)
    dr_ref[...] = (dr + u * k * vd).astype(BF16)
    dk_ref[...] = (dk + u * r * vd).astype(BF16)
    dv_ref[...] = (dv + (per_head(do, heads) * ruk).reshape(width, CHUNK)).astype(BF16)


def time_forward(r, k, v, g, tab, row, ls):
    width, tokens = r.shape
    heads, chunks = width // HEAD, tokens // CHUNK
    piece = pl.BlockSpec((width, CHUNK), lambda c: (0, c))
    return pl.pallas_call(
        functools.partial(mix_forward_kernel, heads),
        grid=(chunks,),
        in_specs=[piece] * 4 + [
            pl.BlockSpec(tab.shape, lambda c: (0, 0)),
            pl.BlockSpec(row.shape, lambda c: (0, 0)),
            pl.BlockSpec((1, CHUNK), lambda c: (0, c)),
        ],
        out_specs=[piece, piece, pl.BlockSpec((1, width, width), lambda c: (c, 0, 0))],
        out_shape=[
            jax.ShapeDtypeStruct((width, tokens), BF16),
            jax.ShapeDtypeStruct((width, tokens), F32),
            jax.ShapeDtypeStruct((chunks, width, width), F32),
        ],
        scratch_shapes=[pltpu.VMEM((width, width), F32)],
        compiler_params=pltpu.CompilerParams(vmem_limit_bytes=48 << 20),
        name="time_forward",
    )(r, k, v, g, tab, row, ls)


def time_backward(r, k, v, g, o, dz, states, tab, row, ls):
    width, tokens = r.shape
    heads, chunks = width // HEAD, tokens // CHUNK
    piece = pl.BlockSpec((width, CHUNK), lambda c: (0, chunks - 1 - c))
    return pl.pallas_call(
        functools.partial(mix_backward_kernel, heads),
        grid=(chunks,),
        in_specs=[piece] * 6 + [
            pl.BlockSpec((1, width, width), lambda c: (chunks - 1 - c, 0, 0)),
            pl.BlockSpec(tab.shape, lambda c: (0, 0)),
            pl.BlockSpec(row.shape, lambda c: (0, 0)),
            pl.BlockSpec((1, CHUNK), lambda c: (0, chunks - 1 - c)),
        ],
        out_specs=[piece] * 4 + [
            pl.BlockSpec((4, width, CHUNK), lambda c: (0, 0, 0)),
            pl.BlockSpec((8, width), lambda c: (0, 0)),
        ],
        out_shape=[jax.ShapeDtypeStruct((width, tokens), BF16)] * 4 + [
            jax.ShapeDtypeStruct((4, width, CHUNK), F32),
            jax.ShapeDtypeStruct((8, width), F32),
        ],
        scratch_shapes=[pltpu.VMEM((width, width), F32)],
        compiler_params=pltpu.CompilerParams(vmem_limit_bytes=48 << 20),
        name="time_backward",
    )(r, k, v, g, o, dz, states, tab, row, ls)


class Moves:
    def __init__(self, sizes):
        self.sizes = sizes
        self.nz = sizes["col"]
        self.x = lax.axis_index("seq")
        self.core = lax.axis_index("core")
        self.z = lax.axis_index("col")

    def shift(self, v, axis, k):
        n = self.sizes[axis]
        return lax.ppermute(v, axis, [(i, (i + k) % n) for i in range(n)])

    def swap(self, v):
        return self.shift(v, "core", 1)

    def cross(self, v):
        return self.shift(v, "seq", 1)

    def hop(self, v, k):
        return self.shift(v, "col", k)

    def ordered(self, at, mine, other, axis):
        return jnp.where(
            at == 0,
            jnp.concatenate([mine, other], axis=axis),
            jnp.concatenate([other, mine], axis=axis),
        )

    def pick(self, v, at):
        return lax.dynamic_index_in_dim(v, at, 0, keepdims=False)

    def gather(self, v):
        half = v.shape[0] // 2
        up, down = [v[:half]], [v[half:]]
        for _ in range(1, self.nz):
            up.append(self.hop(up[-1], 1))
            down.append(self.hop(down[-1], -1))
        rows = []
        for k in range(self.nz):
            a, b = up[k], down[(self.nz - k) % self.nz]
            rows += [a, b, self.swap(a), self.swap(b)]
        return jnp.concatenate(rows, axis=0)

    def scatter_sum(self, p):
        half = p.shape[0] // (self.nz * 4)
        q = p.reshape(self.nz, 2, 2, half, p.shape[1])
        s = [q[k, 0] + self.swap(q[k, 1].astype(BF16)).astype(F32) for k in range(self.nz)]
        low = s[self.nz - 1][0]
        for k in range(self.nz - 2, -1, -1):
            low = self.hop(low.astype(BF16), -1).astype(F32) + s[k][0]
        high = s[1][1]
        for k in range(2, self.nz + 1):
            high = self.hop(high.astype(BF16), 1).astype(F32) + s[k % self.nz][1]
        return jnp.concatenate([low, high], axis=0)

    def small_sum(self, v):
        v = v + self.swap(v)
        total = v
        for k in range(1, self.nz):
            total = total + self.hop(v, k)
        return total

    def over_dp(self, v):
        total = v.astype(F32)
        for k in range(1, self.sizes["dp"]):
            total = total + self.shift(v, "dp", k).astype(F32)
        return total

    def columns(self, stacked):
        nz = self.nz
        mine, other = [], []
        for k in range(nz):
            piece = self.pick(stacked, (self.z + k) % nz)
            piece = self.hop(piece, k) if k else piece
            mine.append(piece)
            other.append(self.cross(piece))
        return jnp.stack(mine), jnp.stack(other)

    def columns_of(self, pair, start, rows):
        mine, other = (v[:, start : start + rows][None] for v in pair)
        v = self.ordered(self.x, mine, other, 0)
        v = v.reshape(2, self.nz, rows, 2, 2, -1)
        v = jnp.where(self.core == 0, v, v[:, :, :, :, ::-1])
        return v.transpose(0, 2, 1, 4, 3, 5).reshape(2 * rows, -1)

    def lines(self, a):
        nz, rows, width = a.shape
        v = a.reshape(nz, rows, 2, 2, width // 4)
        even, odd = v[:, :, :, 0], v[:, :, :, 1]
        keep = jnp.where(self.core == 0, even, odd)
        send = jnp.where(self.core == 0, odd, even)
        both = jnp.stack([keep, self.swap(send)]).reshape(2, nz, rows, width // 2)
        both = self.ordered(self.x, both[None], self.cross(both)[None], 0)
        both = both.transpose(2, 1, 0, 3, 4)
        order = [self.pick(both, (self.z - k) % nz) for k in range(nz)]
        return jnp.stack(order).reshape(nz * 4 * rows, width // 2)

    def return_columns(self, grad):
        nz = self.nz
        rows = grad.shape[0] // 2
        v = grad.reshape(2, rows, nz, 2, 2, -1)
        sent = self.cross(self.pick(v, 1 - self.x).astype(BF16))
        v = self.pick(v, self.x) + sent.astype(F32)
        v = jnp.where(self.core == 0, v, v[:, :, ::-1])
        v = v.transpose(1, 0, 3, 2, 4).reshape(nz, rows, -1).astype(BF16)
        got = [self.hop(v[k], -k) if k else v[k] for k in range(nz)]
        got = jnp.stack([self.over_dp(piece) for piece in got])
        return jnp.stack([self.pick(got, (c - self.z) % nz) for c in range(nz)])

    def return_lines(self, grad):
        nz = self.nz
        rows = grad.shape[0] // (4 * nz)
        v = grad.reshape(nz * 2, 2, rows, -1)
        v = v.transpose(1, 0, 2, 3)
        sent = self.cross(self.pick(v, 1 - self.x).astype(BF16))
        v = (self.pick(v, self.x) + sent.astype(F32)).reshape(nz, 2, rows, 2, 1, -1).astype(BF16)
        v = self.ordered(self.core, v[:, 0], self.swap(v[:, 1]), 3)
        v = self.over_dp(v.reshape(nz, rows, -1))
        return jnp.stack([self.pick(v, (self.z - c) % nz) for c in range(nz)])

    def to_storage(self, v):
        v = v.reshape(2, v.shape[0] // 2, v.shape[1])
        return self.ordered(self.x, self.pick(v, self.x), self.cross(self.pick(v, 1 - self.x)), 1)


def previous(v, keep):
    return jnp.concatenate([jnp.zeros_like(v[:, :1]), v[:, :-1]], axis=1) * keep


def following(v, keep):
    return jnp.concatenate([v[:, 1:] * keep[:, 1:], jnp.zeros_like(v[:, :1])], axis=1)


def norm_stats(v):
    center = jnp.mean(v, axis=0, keepdims=True)
    spread = jnp.mean(jnp.square(v - center), axis=0, keepdims=True)
    return center, lax.rsqrt(spread + norm_eps)


def forward_dot(weight, v):
    return jnp.einsum("oi,it->ot", weight, v, preferred_element_type=F32)


def back_dot(weight, grad):
    return jnp.einsum("oi,ot->it", weight, grad, preferred_element_type=F32)


def weight_dot(grad, v):
    return jnp.einsum("ot,it->oi", grad, v, preferred_element_type=F32)


def mixing_back(grads, coeffs, normed, keep):
    difference = normed - previous(normed, keep)
    straight, shifted, sums = 0.0, 0.0, []
    for grad, coeff in zip(grads, coeffs):
        scaled = grad * coeff
        straight = straight + scaled
        shifted = shifted + (grad - scaled)
        sums.append(jnp.sum(grad * difference, axis=1, keepdims=True))
    return straight + following(shifted, keep), sums


def norm_back_sums(grad, gain, unit):
    scaled = grad * gain
    return jnp.concatenate(
        [jnp.sum(scaled, axis=0, keepdims=True), jnp.sum(scaled * unit, axis=0, keepdims=True)], axis=0
    )


def with_columns(v, columns):
    pad = jnp.zeros((v.shape[0], LANES - len(columns)), v.dtype)
    return jnp.concatenate([v] + list(columns) + [pad], axis=1)


def shards(sizes, tokens, segments, channel_table, w_recept, w_key, w_value, w_gate, w_output,
           ffn_key, ffn_value, ffn_recept, cotangent):
    m = Moves(sizes)
    x = m.x
    count = tokens.shape[1] // 2
    features = tokens.shape[0] * 4 * m.nz

    def mine_of(v, at):
        return lax.dynamic_slice_in_dim(v, at * count, count, axis=v.ndim - 1)

    positions = jnp.arange(segments.shape[0], dtype=jnp.int32)
    earlier = jnp.concatenate([segments[:1], segments[:-1]])
    starts = (positions % SEQ == 0) | (segments != earlier)
    starts = mine_of(starts[None].astype(jnp.int32), x)
    keep = (1 - starts).astype(F32)
    at = jnp.arange(count, dtype=jnp.int32)
    last_start = jnp.max(
        jnp.where((starts > 0) & (at[None, :] <= at[:, None]), at[None, :], 0), axis=1
    )[None]

    table_t = channel_table.T
    table_t = jnp.concatenate(
        [table_t, jnp.zeros((table_t.shape[0], LANES - NPAR), BF16)], axis=1
    )
    here = jnp.concatenate([mine_of(tokens, x), table_t, mine_of(cotangent, x)], axis=1)
    there = jnp.concatenate([mine_of(tokens, 1 - x), table_t, mine_of(cotangent, 1 - x)], axis=1)
    own = m.ordered(x, here, m.cross(there), 0)
    gathered = m.gather(own[:, : count + LANES])
    tok_own = own[:, :count].astype(F32)
    tab_own = own[:, count : count + NPAR].astype(F32)
    cot_own = own[:, count + LANES :].astype(F32)
    all_tokens = gathered[:, :count].astype(F32)
    tab = gathered[:, count : count + NPAR].astype(F32)

    def own_col(n):
        return tab_own[:, n : n + 1]

    def col(n):
        return tab[:, n : n + 1]

    rows = w_recept.shape[1]
    first = m.columns(jnp.concatenate([w_recept, w_key, w_value, w_gate], axis=1))
    w_first = [m.columns_of(first, n * rows, rows) for n in range(4)]

    center_one, inverse_one = norm_stats(all_tokens)
    normed_one = (all_tokens - center_one) * inverse_one * col(0) + col(1)
    shifted_one = previous(normed_one, keep)
    mixes = [
        (normed_one * col(2 + n) + shifted_one * (1.0 - col(2 + n))).astype(BF16) for n in range(4)
    ]
    r, k, v, g = [forward_dot(w_first[n], mixes[n]) for n in range(4)]

    lw = -jnp.exp(own_col(6))
    kernel_tab = jnp.concatenate([lw, own_col(7), own_col(8), own_col(9)], axis=1)
    kernel_row = jnp.broadcast_to(lw.T, (8, lw.shape[0]))
    z, o, states = time_forward(r, k, v, g, kernel_tab, kernel_row, last_start)

    w_out = m.lines(w_output)
    branch = m.scatter_sum(forward_dot(w_out, z))
    h = tok_own + branch
    all_h = m.gather(h.astype(BF16)).astype(F32)

    hidden = ffn_key.shape[1]
    second = m.columns(jnp.concatenate([ffn_recept, ffn_key], axis=1))
    w_rec = m.columns_of(second, 0, rows)
    w_key_ffn = m.columns_of(second, rows, hidden)
    w_val = m.lines(ffn_value)

    center_two, inverse_two = norm_stats(all_h)
    normed_two = (all_h - center_two) * inverse_two * col(10) + col(11)
    shifted_two = previous(normed_two, keep)
    e_k, e_r = [
        (normed_two * col(n) + shifted_two * (1.0 - col(n))).astype(BF16) for n in (12, 13)
    ]
    rr = forward_dot(w_rec, e_r)
    gate = jax.nn.sigmoid(rr)
    dvv = (cot_own * gate).astype(BF16)
    all_dvv = m.gather(dvv)
    kk = jax.nn.relu(forward_dot(w_key_ffn, e_k))
    act = jnp.square(kk).astype(BF16)
    vv = m.scatter_sum(forward_dot(w_val, act))
    mixed = (h + gate * vv).astype(BF16)
    drr = (cot_own * vv * gate * (1.0 - gate)).astype(BF16)

    grad_value = m.return_lines(weight_dot(all_dvv, act))
    dkk = (back_dot(w_val, all_dvv) * 2.0 * kk).astype(BF16)
    grad_key = m.return_columns(weight_dot(dkk, e_k))
    grad_rec = m.return_columns(weight_dot(drr, e_r))
    dn_two, sums_two = mixing_back(
        [back_dot(w_key_ffn, dkk), back_dot(w_rec, drr)], [col(12), col(13)], normed_two, keep
    )
    unit_all_two = (all_h - center_two) * inverse_two
    totals_two = m.small_sum(norm_back_sums(dn_two, col(10), unit_all_two)) / features
    summed_two = m.scatter_sum(with_columns(dn_two, sums_two))
    dn_two_own = summed_two[:, :count]
    unit_two = (h - center_two) * inverse_two
    gain_two = jnp.sum(dn_two_own * unit_two, axis=1, keepdims=True)
    bias_two = jnp.sum(dn_two_own, axis=1, keepdims=True)
    dh = cot_own + inverse_two * (
        dn_two_own * own_col(10) - totals_two[0:1] - unit_two * totals_two[1:2]
    )

    all_dh = m.gather(dh.astype(BF16))
    dz = back_dot(w_out, all_dh)
    grad_output = m.return_lines(weight_dot(all_dh, z))
    *dps, acc, row_acc = time_backward(
        r, k, v, g, o, dz, states, kernel_tab, kernel_row, last_start
    )
    acc = jnp.sum(acc, axis=2)
    grad_rows = [
        ((acc[0] + row_acc[0]) * lw[:, 0])[:, None],
        acc[1][:, None],
        acc[2][:, None],
        acc[3][:, None],
    ]
    grads_time = [m.return_columns(weight_dot(dps[n], mixes[n])) for n in range(4)]
    dn_one, sums_one = mixing_back(
        [back_dot(w_first[n], dps[n]) for n in range(4)],
        [col(2 + n) for n in range(4)],
        normed_one,
        keep,
    )
    unit_all_one = (all_tokens - center_one) * inverse_one
    totals_one = m.small_sum(norm_back_sums(dn_one, col(0), unit_all_one)) / features
    summed_one = m.scatter_sum(with_columns(dn_one, sums_one))
    dn_one_own = summed_one[:, :count]
    unit_one = (tok_own - center_one) * inverse_one
    gain_one = jnp.sum(dn_one_own * unit_one, axis=1, keepdims=True)
    bias_one = jnp.sum(dn_one_own, axis=1, keepdims=True)
    grad_tokens = dh + inverse_one * (
        dn_one_own * own_col(0) - totals_one[0:1] - unit_one * totals_one[1:2]
    )

    sums = with_columns(
        gain_one,
        [bias_one, summed_one[:, count : count + 4]]
        + grad_rows
        + [gain_two, bias_two, summed_two[:, count : count + 2]],
    )[:, :NPAR]
    sums = sums.reshape(2, sums.shape[0] // 2, NPAR)
    table = m.pick(sums, x) + m.cross(m.pick(sums, 1 - x))
    table = m.over_dp(table).T
    return (
        m.to_storage(mixed),
        m.to_storage(grad_tokens),
        table,
        grads_time[0],
        grads_time[1],
        grads_time[2],
        grads_time[3],
        grad_output,
        grad_key,
        grad_value,
        grad_rec,
    )


def solution(mesh):
    sizes = {"dp": mesh.shape["dp"], "seq": 2, "core": mesh.shape["row"] // 2, "col": mesh.shape["col"]}
    fine = Mesh(mesh.devices.reshape(tuple(sizes.values())), tuple(sizes))
    both = P(("col", "seq", "core"), "dp")
    weight = P(None, ("seq", "core"), "col")
    table = P(None, ("col", "seq", "core"))
    return jax.shard_map(
        functools.partial(shards, sizes),
        mesh=fine,
        in_specs=(both, P("dp"), table) + (weight,) * 8 + (both,),
        out_specs=(both, both, table) + (weight,) * 8,
        check_vma=False,
    )
```
